1024 devices in a mesh: row: 64 (over z, core), vec: 16 (over y, x).
Axes of the slice: x: 4, y: 4, z: 32, core: 2. Of those that a mesh axis runs over, the one named last changes fastest.
Arguments:
- vectors: float32 [131072, 2048], P('row', 'vec'), may hold values from -6 to 6
- band_head: float32 [128, 131072], P(None, 'row'), may hold values from -0.125 to 0.125
- band_tail: float32 [128, 32768], P(None, 'row'), may hold values from -0.125 to 0.125
- band_factor: float32 [64, 128, 128], P('row'), may hold values from -0.5 to 0.5
- panel_vectors: bfloat16 [2, 512, 131072], P(None, 'vec', 'row'), may hold values from -0.03125 to 0.03125
- panel_factor: float32 [2, 512, 512], replicated, may hold values from -0.25 to 0.25
Outputs:
- result: float32 [131072, 2048], P('row', 'vec')
The draws below stay inside these ranges and needn't reach their ends.
All inputs are finite; a program needn't handle non-finite values.
Results may differ from the reference program's by a relative error of at most 0.0003.
Values may be sent and summed in bfloat16 or wider, within the bound.
No kernel may reach another device: no remote copies, remote signals or barrier semaphores. Data moves between devices by JAX's collectives and lax.ppermute only.
A program may use at most 64 MiB of HBM per device.

```python
import jax
import jax.numpy as jnp
import numpy as np
from jax import lax

ROW_DEV = 2048
MARGIN = 512
BANDW = 128
PANEL = 512
PANELS = 2
NROWS = 131072
NVEC = 2048
N_ROW = 64


def shard_levels(own_key, extent, pieces, smallest, top_value):
    def one(axis_at, blocks):
        steps = jax.random.uniform(jax.random.fold_in(jax.random.fold_in(own_key, 6), axis_at), (blocks,), jnp.float32, smallest / len(pieces), top_value / len(pieces))
        return jnp.repeat(jnp.exp(steps), extent[axis_at] // blocks).reshape((-1,) + (1,) * (len(extent) - axis_at - 1))

    loudness = one(*pieces[0])
    for cut in pieces[1:]:
        loudness = loudness * one(*cut)
    return loudness


def gaussian(rng, extent, scale, reach, shards=(), dtype=jnp.bfloat16):
    result = jax.random.normal(rng, extent, jnp.float32) * scale
    if len(shards) > 0:
        result = shard_levels(rng, extent, shards, -0.22, 0.18) * result
    return jnp.clip(result, min=-reach, max=reach).astype(dtype)


def setup_inputs(seed: int = 0) -> dict:
    key_of = jax.random.split(jax.random.key(seed), 7)
    vectors = gaussian(key_of[0], (NROWS, NVEC), 1.0, 6.0, ((0, 64), (1, 16)), jnp.float32)
    band_head = gaussian(key_of[1], (BANDW, NROWS), (ROW_DEV + MARGIN) ** -0.5, 0.125, ((1, 64),), jnp.float32)
    band_tail = gaussian(key_of[2], (BANDW, N_ROW * MARGIN), (ROW_DEV + MARGIN) ** -0.5, 0.125, ((1, 64),), jnp.float32)
    band_factor = gaussian(key_of[3], (N_ROW, BANDW, BANDW), BANDW ** -0.5, 0.5, ((0, 64),), jnp.float32)
    panel_vectors = gaussian(key_of[4], (PANELS, PANEL, NROWS), (NROWS // 4) ** -0.5, 0.03125, ((1, 16), (2, 64)))
    panel_factor = gaussian(key_of[5], (PANELS, PANEL, PANEL), PANEL ** -0.5, 0.25, (), jnp.float32)
    return dict(vectors=vectors, band_head=band_head, band_tail=band_tail, band_factor=band_factor, panel_vectors=panel_vectors, panel_factor=panel_factor)


HIGHEST = lax.Precision.HIGHEST


def product(left, right):
    return jnp.dot(left, right, precision=HIGHEST, preferred_element_type=jnp.float32)


def reference(vectors, band_head, band_tail, band_factor, panel_vectors, panel_factor):
    blocks = vectors.reshape(N_ROW, ROW_DEV, NVEC)
    heads = band_head.reshape(BANDW, N_ROW, ROW_DEV).transpose(1, 0, 2)
    tails = band_tail.reshape(BANDW, N_ROW, MARGIN).transpose(1, 0, 2)
    tails_next = jnp.roll(tails, -1, axis=0)
    factors = jnp.triu(band_factor)
    for sweep_phase in range(2):
        owners = np.arange(sweep_phase, N_ROW, 2)
        followers = (owners + 1) % N_ROW
        owned_rows = blocks[owners]
        following = blocks[followers, :MARGIN]
        head_sel = heads[owners]
        tail_sel = tails_next[owners]
        projection = jnp.einsum("gkr,grc->gkc", head_sel, owned_rows, precision=HIGHEST) + jnp.einsum("gkr,grc->gkc", tail_sel, following, precision=HIGHEST)
        weights = jnp.einsum("gkj,gjc->gkc", factors[owners], projection, precision=HIGHEST)
        owned_new = owned_rows - jnp.einsum("gkr,gkc->grc", head_sel, weights, precision=HIGHEST)
        following_new = following - jnp.einsum("gkr,gkc->grc", tail_sel, weights, precision=HIGHEST)
        blocks = blocks.at[owners].set(owned_new)
        blocks = blocks.at[followers, :MARGIN].set(following_new)
    current = blocks.reshape(NROWS, NVEC)
    panel_tri = jnp.triu(panel_factor)
    for panel_index in range(PANELS):
        panel_rows = panel_vectors[panel_index].astype(jnp.float32)
        summed = product(panel_rows, current)
        weights = product(panel_tri[panel_index], summed)
        current = current - product(panel_rows.T, weights)
    return current
```

```python
import jax
import jax.numpy as jnp
from jax import lax
from jax.sharding import Mesh
from jax.sharding import PartitionSpec as P

ROW = ("far", "near", "core")
NEAR = ("near", "core")
CHIPS = ("far", "near")
HIGHEST = lax.Precision.HIGHEST
F32 = jnp.float32
BF16 = jnp.bfloat16


def product(left, right):
    return jnp.dot(left, right, precision=HIGHEST, preferred_element_type=F32)


def product_t(left, right):
    return lax.dot_general(left, right, (((0,), (0,)), ((), ())), precision=HIGHEST, preferred_element_type=F32)


def product_nt(left, right):
    return lax.dot_general(left, right, (((1,), (1,)), ((), ())), precision=HIGHEST, preferred_element_type=F32)


def thirds(array):
    high = lax.reduce_precision(array, 8, 7)
    rest = array - high
    mid = lax.reduce_precision(rest, 8, 7)
    low = rest - mid
    return jnp.concatenate([high.astype(BF16), mid.astype(BF16), low.astype(BF16)], axis=1)


def fold(wide):
    width = wide.shape[1] // 3
    return wide[:, :width] + (wide[:, width : 2 * width] + wide[:, 2 * width :])


def to_everyone(array, axis):
    copies = jnp.broadcast_to(array, (lax.axis_size(axis), *array.shape))
    return lax.all_to_all(copies, axis, split_axis=0, concat_axis=0, tiled=True)


def swapped(array):
    return lax.ppermute(array, "core", [(0, 1), (1, 0)])


def halves(array):
    middle = array.shape[0] // 2
    return array[:middle], array[middle:]


def core_share(partial, first):
    low, high = halves(partial)
    return jnp.where(first, low, high) + swapped(jnp.where(first, high, low))


def joined(mine, other, first):
    return jnp.concatenate([jnp.where(first, mine, other), jnp.where(first, other, mine)], axis=0)


def summed_over_rows(part_a, part_b, first):
    group = lax.axis_size("near")
    width = part_a.shape[1]
    share_a, share_b = core_share(part_a, first), core_share(part_b, first)
    cut = share_a.shape[0] // group
    blocks = jnp.concatenate([share_a.reshape(group, -1, width), share_b.reshape(group, -1, width)], axis=1)
    share = jnp.sum(lax.all_to_all(blocks, "near", split_axis=0, concat_axis=0, tiled=True), axis=0)
    share = jnp.sum(to_everyone(share, "far"), axis=0)
    mine = to_everyone(share, "near")
    other = swapped(mine)
    sum_a = joined(mine[:, :cut].reshape(-1, width), other[:, :cut].reshape(-1, width), first)
    sum_b = joined(mine[:, cut:].reshape(-1, width), other[:, cut:].reshape(-1, width), first)
    return sum_a, sum_b


def on_device(vectors, band_head, band_tail, band_factor, panel_vectors, panel_factor):
    margin = band_tail.shape[1]
    own_chunk, width = panel_vectors.shape[1], vectors.shape[1]
    depth = panel_factor.shape[1]
    even = lax.axis_index("core") == 0
    n = lax.axis_size(ROW)

    panel0 = to_everyone(panel_vectors[0], "vec").reshape(depth, -1)
    panel1 = to_everyone(panel_vectors[1], "vec").reshape(depth, -1)

    factor = jnp.triu(band_factor[0])
    own = product(band_head, vectors)
    tail = product(band_tail, vectors[:margin])
    cross = product_nt(band_tail, band_head[:, :margin])
    tail_next = lax.ppermute(tail, ROW, [(i + 1, i) for i in range(0, n, 2)])
    weights_a = product(factor, own + tail_next)
    weights_a_prev = lax.ppermute(weights_a, ROW, [(i, i + 1) for i in range(0, n, 2)])
    tail_b = tail - product(cross, weights_a)
    tail_b_next = lax.ppermute(tail_b, ROW, [(i, (i - 1) % n) for i in range(0, n, 2)])
    weights_b = product(factor, own - product_t(cross, weights_a_prev) + tail_b_next)
    weights_b_prev = lax.ppermute(weights_b, ROW, [(i, (i + 1) % n) for i in range(1, n, 2)])
    weights_own = jnp.where(even, weights_a, weights_b)
    weights_prev = jnp.where(even, weights_b_prev, weights_a_prev)
    current = vectors - product_t(band_head, weights_own)
    top = current[:margin] - product_t(band_tail, weights_prev)
    current = jnp.concatenate([top, current[margin:]], axis=0)

    split = thirds(current)
    part0 = fold(jnp.dot(panel0, split, preferred_element_type=F32))
    gram = lax.dot_general(panel_vectors[1], panel0, (((1,), (1,)), ((), ())), preferred_element_type=F32)
    pieces = depth // width
    gram_rows = jnp.concatenate([gram[:, i * width : (i + 1) * width] for i in range(pieces)], axis=0)
    mixed = jnp.concatenate(
        [part0[: depth // 2], gram_rows[: width // 2], part0[depth // 2 :], gram_rows[width // 2 :]], axis=0
    )
    part1 = fold(jnp.dot(panel1, split, preferred_element_type=F32))
    mixed_sum, sum1 = summed_over_rows(mixed, part1, even)
    low, high = halves(mixed_sum)
    sum0 = jnp.concatenate([low[: depth // 2], high[: depth // 2], low[depth // 2 :], high[depth // 2 :]], axis=0)

    gram_own = jnp.concatenate([sum0[depth + i * own_chunk : depth + (i + 1) * own_chunk] for i in range(pieces)], axis=1)
    gram_all = to_everyone(gram_own, "vec").reshape(depth, depth)
    tri = jnp.triu(panel_factor)
    w0 = product(tri[0], sum0[:depth])
    w1 = product(tri[1], sum1 - product(gram_all, w0))

    def spread(panel, w):
        return fold(lax.dot_general(panel, thirds(w), (((0,), (0,)), ((), ())), preferred_element_type=F32))

    return current - spread(panel0, w0) - spread(panel1, w1)


def solution(mesh):
    devices = mesh.devices.reshape(4, 8, 2, mesh.shape["vec"])
    split = Mesh(devices, ("far", "near", "core", "vec"))
    return jax.shard_map(
        on_device,
        mesh=split,
        in_specs=(
            P(ROW, "vec"),
            P(None, ROW),
            P(None, ROW),
            P(ROW, None, None),
            P(None, "vec", ROW),
            P(),
        ),
        out_specs=P(ROW, "vec"),
        check_vma=False,
    )
```

```python
import functools

import jax
import jax.numpy as jnp
from jax import lax
from jax.experimental import pallas as pl
from jax.experimental.pallas import tpu as pltpu
from jax.sharding import Mesh
from jax.sharding import PartitionSpec as P

ROW = ("far", "near", "core")
HIGHEST = lax.Precision.HIGHEST
F32 = jnp.float32
BF16 = jnp.bfloat16


def product(left, right):
    return jnp.dot(left, right, precision=HIGHEST, preferred_element_type=F32)


def product_t(left, right):
    return lax.dot_general(left, right, (((0,), (0,)), ((), ())), precision=HIGHEST, preferred_element_type=F32)


def product_nt(left, right):
    return lax.dot_general(left, right, (((1,), (1,)), ((), ())), precision=HIGHEST, preferred_element_type=F32)


def store_thirds(target, array):
    width = array.shape[1]
    high = array.astype(BF16)
    rest = array - high.astype(F32)
    mid = rest.astype(BF16)
    target[:, :width] = high
    target[:, width : 2 * width] = mid
    target[:, 2 * width :] = (rest - mid.astype(F32)).astype(BF16)


def fold(wide):
    width = wide.shape[1] // 3
    return wide[:, :width] + (wide[:, width : 2 * width] + wide[:, 2 * width :])


def to_everyone(array, axis):
    copies = jnp.broadcast_to(array, (lax.axis_size(axis), *array.shape))
    return lax.all_to_all(copies, axis, split_axis=0, concat_axis=0, tiled=True)


def swapped(array):
    return lax.ppermute(array, "core", [(0, 1), (1, 0)])


def project_kernel(core_ref, panel_ref, own_ref, current_ref, send_ref, keep_ref, split):
    del core_ref
    step = pl.program_id(0)

    @pl.when(step == 0)
    def _():
        store_thirds(split, current_ref[...])

    rows = panel_ref.shape[0] * panel_ref.shape[1]
    own, width = own_ref.shape[0], current_ref.shape[1]
    tiles = rows // width
    gram_end = rows + own * tiles
    panel = panel_ref[...].reshape(rows, panel_ref.shape[2])
    part = fold(jnp.dot(panel, split[...], preferred_element_type=F32))
    for which, out_ref in enumerate((send_ref, keep_ref)):

        @pl.when(step == 2 * which)
        def _(out_ref=out_ref):
            out_ref[:rows] = part
            gram = lax.dot_general(own_ref[...], panel, (((1,), (1,)), ((), ())), preferred_element_type=F32)
            for t in range(tiles):
                out_ref[rows + own * t : rows + own * (t + 1)] = gram[:, width * t : width * (t + 1)]

        @pl.when(step == 2 * which + 1)
        def _(out_ref=out_ref):
            out_ref[gram_end:] = part


def project(core, panels, panel_vectors, current):
    sources, _, own, depth_rows = panels.shape
    rows, width = sources // 2 * own, current.shape[1]
    total = 2 * rows + own * (rows // width)
    whole = pl.BlockSpec((total, width), lambda i, c: (0, 0))
    flops = 2 * 2 * sources * own * depth_rows * width * 3
    return pl.pallas_call(
        project_kernel,
        out_shape=[jax.ShapeDtypeStruct((total, width), F32)] * 2,
        grid_spec=pltpu.PrefetchScalarGridSpec(
            num_scalar_prefetch=1,
            grid=(4,),
            in_specs=[
                pl.BlockSpec(
                    (sources // 2, None, own, depth_rows),
                    lambda i, c: (jnp.where(i < 2, 1 - c[0], c[0]), i % 2, 0, 0),
                ),
                pl.BlockSpec((None, own, depth_rows), lambda i, c: (1, 0, 0)),
                pl.BlockSpec(current.shape, lambda i, c: (0, 0)),
            ],
            out_specs=[whole, whole],
            scratch_shapes=[pltpu.VMEM((depth_rows, 3 * width), BF16)],
        ),
        cost_estimate=pl.CostEstimate(flops=flops, bytes_accessed=panels.size * 2 + current.size * 4, transcendentals=0),
        name="project",
    )(core, panels, panel_vectors, current)


def apply_kernel(first_row, corrections, core_ref, mine_ref, other_ref, factor_ref, panel_ref, current_ref, *refs):
    correction_refs, (weights_ref, out_ref, total, split) = refs[:corrections], refs[corrections:]
    depth = factor_ref.shape[0]
    half = depth // 2

    @pl.when(pl.program_id(0) == 0)
    def _():
        for which, (low_ref, high_ref) in enumerate(((mine_ref, other_ref), (other_ref, mine_ref))):

            @pl.when(core_ref[0] == which)
            def _(low_ref=low_ref, high_ref=high_ref):
                total[:half] = low_ref[first_row : first_row + half]
                total[half:] = high_ref[first_row : first_row + half]

        wanted = total[...]
        if corrections:
            wanted = wanted - (correction_refs[0][...] + correction_refs[1][...])
        row = lax.broadcasted_iota(jnp.int32, (depth, depth), 0)
        column = lax.broadcasted_iota(jnp.int32, (depth, depth), 1)
        factor = jnp.where(row <= column, factor_ref[...], 0.0)
        weights = product(factor, wanted)
        weights_ref[...] = weights
        store_thirds(split, weights)

    panel = panel_ref[...].reshape(depth, panel_ref.shape[2])
    update = lax.dot_general(panel, split[...], (((0,), (0,)), ((), ())), preferred_element_type=F32)
    out_ref[...] = current_ref[...] - fold(update)


def apply_panel(core, mine, other, panel_factor, panels, current, index, first_row, corrections=()):
    sources, _, own, n_rows = panels.shape
    depth, width = panel_factor.shape[1], current.shape[1]
    steps = 4
    block = n_rows // steps
    whole = lambda array: pl.BlockSpec(array.shape, lambda i, c: (0, 0))
    flops = 2 * n_rows * depth * width * 3 + 2 * depth * depth * width * 6
    return pl.pallas_call(
        functools.partial(apply_kernel, first_row, len(corrections)),
        out_shape=[jax.ShapeDtypeStruct((depth, width), F32), jax.ShapeDtypeStruct(current.shape, F32)],
        grid_spec=pltpu.PrefetchScalarGridSpec(
            num_scalar_prefetch=1,
            grid=(steps,),
            in_specs=[
                whole(mine),
                whole(other),
                pl.BlockSpec((None, depth, depth), lambda i, c: (index, 0, 0)),
                pl.BlockSpec((sources, None, own, block), lambda i, c: (0, index, 0, i)),
                pl.BlockSpec((block, width), lambda i, c: (i, 0)),
                *[whole(array) for array in corrections],
            ],
            out_specs=[
                pl.BlockSpec((depth, width), lambda i, c: (0, 0)),
                pl.BlockSpec((block, width), lambda i, c: (i, 0)),
            ],
            scratch_shapes=[pltpu.VMEM((depth, width), F32), pltpu.VMEM((depth, 3 * width), BF16)],
        ),
        cost_estimate=pl.CostEstimate(flops=flops, bytes_accessed=panels.size + current.size * 8, transcendentals=0),
        name="apply_panel",
    )(core, mine, other, panel_factor, panels, current, *corrections)


def couple_kernel(core_ref, gram_ref, weights_ref, out_ref):
    sources, rows, width = gram_ref.shape
    depth = weights_ref.shape[0]
    tiles = depth // 2 // width
    own = rows // tiles
    result = None
    for t in range(tiles):
        gram = gram_ref[:, own * t : own * (t + 1)].reshape(sources * own, width)
        start = pl.multiple_of(core_ref[0] * (depth // 2) + width * t, width)
        term = product(gram, weights_ref[pl.ds(start, width)])
        result = term if result is None else result + term
    out_ref[...] = result


def couple(core, gram, weights):
    return pl.pallas_call(
        couple_kernel,
        out_shape=jax.ShapeDtypeStruct(weights.shape, F32),
        in_specs=[pl.BlockSpec(memory_space=pltpu.SMEM)] + [pl.BlockSpec(memory_space=pltpu.VMEM)] * 2,
        out_specs=pl.BlockSpec(memory_space=pltpu.VMEM),
        cost_estimate=pl.CostEstimate(flops=weights.size * weights.shape[0] * 6, bytes_accessed=gram.size * 4, transcendentals=0),
        name="couple",
    )(core, gram, weights)


def on_device(vectors, band_head, band_tail, band_factor, panel_vectors, panel_factor):
    margin = band_tail.shape[1]
    width = vectors.shape[1]
    depth = panel_factor.shape[1]
    core_index = lax.axis_index("core")
    even = core_index == 0
    core = core_index.astype(jnp.int32).reshape(1)
    n = lax.axis_size(ROW)

    panels = to_everyone(panel_vectors, "vec")

    factor = jnp.triu(band_factor[0])
    own = product(band_head, vectors)
    tail = product(band_tail, vectors[:margin])
    cross = product_nt(band_tail, band_head[:, :margin])
    tail_next = lax.ppermute(tail, ROW, [(i + 1, i) for i in range(0, n, 2)])
    weights_a = product(factor, own + tail_next)
    weights_a_prev = lax.ppermute(weights_a, ROW, [(i, i + 1) for i in range(0, n, 2)])
    tail_b = tail - product(cross, weights_a)
    tail_b_next = lax.ppermute(tail_b, ROW, [(i, (i - 1) % n) for i in range(0, n, 2)])
    weights_b = product(factor, own - product_t(cross, weights_a_prev) + tail_b_next)
    weights_b_prev = lax.ppermute(weights_b, ROW, [(i, (i + 1) % n) for i in range(1, n, 2)])
    weights_own = jnp.where(even, weights_a, weights_b)
    weights_prev = jnp.where(even, weights_b_prev, weights_a_prev)
    current = vectors - product_t(band_head, weights_own)
    top = current[:margin] - product_t(band_tail, weights_prev)
    current = jnp.concatenate([top, current[margin:]], axis=0)

    send, keep = project(core, panels, panel_vectors, current)
    group = lax.axis_size("near")
    blocks = (keep + swapped(send)).reshape(group, -1, width)
    share = jnp.sum(lax.all_to_all(blocks, "near", split_axis=0, concat_axis=0, tiled=True), axis=0)
    share = jnp.sum(to_everyone(share, "far"), axis=0)
    mine = to_everyone(share, "near").reshape(-1, width)
    half = depth // 2
    gram_end = mine.shape[0] - half
    gram = to_everyone(mine[half:gram_end], "vec")
    other = swapped(mine)

    weights0, current = apply_panel(core, mine, other, panel_factor, panels, current, 0, 0)
    coupled = couple(core, gram, weights0)
    corrections = (coupled, swapped(coupled))
    _, result = apply_panel(core, mine, other, panel_factor, panels, current, 1, gram_end, corrections)
    return result


def solution(mesh):
    devices = mesh.devices.reshape(4, 8, 2, mesh.shape["vec"])
    split = Mesh(devices, ("far", "near", "core", "vec"))
    return jax.shard_map(
        on_device,
        mesh=split,
        in_specs=(
            P(ROW, "vec"),
            P(None, ROW),
            P(None, ROW),
            P(ROW, None, None),
            P(None, "vec", ROW),
            P(),
        ),
        out_specs=P(ROW, "vec"),
        check_vma=False,
    )
```

```python
import functools

import jax
import jax.numpy as jnp
from jax import lax
from jax.experimental import pallas as pl
from jax.experimental.pallas import tpu as pltpu
from jax.sharding import Mesh
from jax.sharding import PartitionSpec as P

ROW = ("far", "near", "core")
HIGHEST = lax.Precision.HIGHEST
F32 = jnp.float32
BF16 = jnp.bfloat16


def product(left, right):
    return jnp.dot(left, right, precision=HIGHEST, preferred_element_type=F32)


def product_t(left, right):
    return lax.dot_general(left, right, (((0,), (0,)), ((), ())), precision=HIGHEST, preferred_element_type=F32)


def product_nt(left, right):
    return lax.dot_general(left, right, (((1,), (1,)), ((), ())), precision=HIGHEST, preferred_element_type=F32)


def store_pieces(target, array):
    width = array.shape[1]
    high = array.astype(BF16)
    target[:, :width] = high
    target[:, width:] = (array - high.astype(F32)).astype(BF16)


def fold(wide):
    width = wide.shape[1] // 2
    return wide[:, :width] + wide[:, width:]


def to_everyone(array, axis):
    copies = jnp.broadcast_to(array, (lax.axis_size(axis), *array.shape))
    return lax.all_to_all(copies, axis, split_axis=0, concat_axis=0, tiled=True)


def swapped(array):
    return lax.ppermute(array, "core", [(0, 1), (1, 0)])


def copies_kernel(source_ref, out_ref, sems):
    moves = [pltpu.make_async_copy(source_ref, out_ref.at[i], sems.at[i]) for i in range(out_ref.shape[0])]
    for move in moves:
        move.start()
    for move in moves:
        move.wait()


def copies(array, count):
    return pl.pallas_call(
        copies_kernel,
        out_shape=jax.ShapeDtypeStruct((count, *array.shape), array.dtype),
        in_specs=[pl.BlockSpec(memory_space=pltpu.VMEM)],
        out_specs=pl.BlockSpec(memory_space=pl.ANY),
        scratch_shapes=[pltpu.SemaphoreType.DMA((count,))],
        name="copies",
    )(array)


def project_kernel(core_ref, panel_ref, own_ref, current_ref, send_ref, keep_ref, split):
    del core_ref
    step = pl.program_id(0)

    @pl.when(step == 0)
    def _():
        store_pieces(split, current_ref[...])

    rows = panel_ref.shape[0] * panel_ref.shape[1]
    own, width = own_ref.shape[0], current_ref.shape[1]
    tiles = rows // width
    gram_end = rows + own * tiles
    panel = panel_ref[...].reshape(rows, panel_ref.shape[2])
    part = fold(jnp.dot(panel, split[...], preferred_element_type=F32))
    for which, out_ref in enumerate((send_ref, keep_ref)):

        @pl.when(step == 2 * which)
        def _(out_ref=out_ref):
            out_ref[:rows] = part
            gram = lax.dot_general(own_ref[...], panel, (((1,), (1,)), ((), ())), preferred_element_type=F32)
            for t in range(tiles):
                out_ref[rows + own * t : rows + own * (t + 1)] = gram[:, width * t : width * (t + 1)]

        @pl.when(step == 2 * which + 1)
        def _(out_ref=out_ref):
            out_ref[gram_end:] = part


def project(core, panels, panel_vectors, current):
    sources, _, own, depth_rows = panels.shape
    rows, width = sources // 2 * own, current.shape[1]
    total = 2 * rows + own * (rows // width)
    whole = pl.BlockSpec((total, width), lambda i, c: (0, 0))
    flops = 2 * 2 * sources * own * depth_rows * width * 2
    return pl.pallas_call(
        project_kernel,
        out_shape=[jax.ShapeDtypeStruct((total, width), F32)] * 2,
        grid_spec=pltpu.PrefetchScalarGridSpec(
            num_scalar_prefetch=1,
            grid=(4,),
            in_specs=[
                pl.BlockSpec(
                    (sources // 2, None, own, depth_rows),
                    lambda i, c: (jnp.where(i < 2, 1 - c[0], c[0]), i % 2, 0, 0),
                ),
                pl.BlockSpec((None, own, depth_rows), lambda i, c: (1, 0, 0)),
                pl.BlockSpec(current.shape, lambda i, c: (0, 0)),
            ],
            out_specs=[whole, whole],
            scratch_shapes=[pltpu.VMEM((depth_rows, 2 * width), BF16)],
        ),
        cost_estimate=pl.CostEstimate(flops=flops, bytes_accessed=panels.size * 2 + current.size * 4, transcendentals=0),
        name="project",
    )(core, panels, panel_vectors, current)


def weigh(first_row, core_ref, mine_ref, other_ref, factor_ref, total, corrections=()):
    depth = factor_ref.shape[0]
    half = depth // 2
    for which, (low_ref, high_ref) in enumerate(((mine_ref, other_ref), (other_ref, mine_ref))):

        @pl.when(core_ref[0] == which)
        def _(low_ref=low_ref, high_ref=high_ref):
            total[:half] = low_ref[first_row : first_row + half]
            total[half:] = high_ref[first_row : first_row + half]

    wanted = total[...]
    if corrections:
        wanted = wanted - (corrections[0][...] + corrections[1][...])
    row = lax.broadcasted_iota(jnp.int32, (depth, depth), 0)
    column = lax.broadcasted_iota(jnp.int32, (depth, depth), 1)
    return product(jnp.where(row <= column, factor_ref[...], 0.0), wanted)


def first_weights_kernel(core_ref, mine_ref, other_ref, factor_ref, weights_ref, total):
    weights_ref[...] = weigh(0, core_ref, mine_ref, other_ref, factor_ref, total)


def first_weights(core, mine, other, panel_factor):
    depth, width = panel_factor.shape[1], mine.shape[1]
    whole = pl.BlockSpec(mine.shape, lambda i, c: (0, 0))
    return pl.pallas_call(
        first_weights_kernel,
        out_shape=jax.ShapeDtypeStruct((depth, width), F32),
        grid_spec=pltpu.PrefetchScalarGridSpec(
            num_scalar_prefetch=1,
            grid=(1,),
            in_specs=[whole, whole, pl.BlockSpec((None, depth, depth), lambda i, c: (0, 0, 0))],
            out_specs=pl.BlockSpec((depth, width), lambda i, c: (0, 0)),
            scratch_shapes=[pltpu.VMEM((depth, width), F32)],
        ),
        cost_estimate=pl.CostEstimate(flops=2 * depth * depth * width * 6, bytes_accessed=4 * depth * depth, transcendentals=0),
        name="first_weights",
    )(core, mine, other, panel_factor)


def update(panel_ref, split, current_ref, out_ref):
    panel = panel_ref[...].reshape(split.shape[0], panel_ref.shape[2])
    wide = lax.dot_general(panel, split[...], (((0,), (0,)), ((), ())), preferred_element_type=F32)
    out_ref[...] = current_ref[...] - fold(wide)


def apply_kernel(weights_ref, panel_ref, current_ref, out_ref, split):
    @pl.when(pl.program_id(0) == 0)
    def _():
        store_pieces(split, weights_ref[...])

    update(panel_ref, split, current_ref, out_ref)


STEPS = 4


def apply_first(weights, panels, current):
    sources, _, own, n_rows = panels.shape
    depth, width = weights.shape
    block = n_rows // STEPS
    rows = pl.BlockSpec((block, width), lambda i: (i, 0))
    return pl.pallas_call(
        apply_kernel,
        out_shape=jax.ShapeDtypeStruct(current.shape, F32),
        grid=(STEPS,),
        in_specs=[
            pl.BlockSpec((depth, width), lambda i: (0, 0)),
            pl.BlockSpec((sources, None, own, block), lambda i: (0, 0, 0, i)),
            rows,
        ],
        out_specs=rows,
        scratch_shapes=[pltpu.VMEM((depth, 2 * width), BF16)],
        cost_estimate=pl.CostEstimate(
            flops=2 * n_rows * depth * width * 2, bytes_accessed=panels.size + current.size * 8, transcendentals=0
        ),
        name="apply_first",
    )(weights, panels, current)


def finish_kernel(
    first_row, core_ref, mine_ref, other_ref, factor_ref, own_part, other_part, panel_ref, current_ref, out_ref, total, split
):
    @pl.when(pl.program_id(0) == 0)
    def _():
        store_pieces(
            split, weigh(first_row, core_ref, mine_ref, other_ref, factor_ref, total, (own_part, other_part))
        )

    update(panel_ref, split, current_ref, out_ref)


def finish(core, mine, other, panel_factor, own_part, other_part, panels, current, first_row):
    sources, _, own, n_rows = panels.shape
    depth, width = own_part.shape
    block = n_rows // STEPS
    whole = lambda array: pl.BlockSpec(array.shape, lambda i, c: (0, 0))
    rows = pl.BlockSpec((block, width), lambda i, c: (i, 0))
    flops = 2 * n_rows * depth * width * 2 + 2 * depth * depth * width * 6
    return pl.pallas_call(
        functools.partial(finish_kernel, first_row),
        out_shape=jax.ShapeDtypeStruct(current.shape, F32),
        grid_spec=pltpu.PrefetchScalarGridSpec(
            num_scalar_prefetch=1,
            grid=(STEPS,),
            in_specs=[
                whole(mine),
                whole(other),
                pl.BlockSpec((None, depth, depth), lambda i, c: (1, 0, 0)),
                whole(own_part),
                whole(other_part),
                pl.BlockSpec((sources, None, own, block), lambda i, c: (0, 1, 0, i)),
                rows,
            ],
            out_specs=rows,
            scratch_shapes=[pltpu.VMEM((depth, width), F32), pltpu.VMEM((depth, 2 * width), BF16)],
        ),
        cost_estimate=pl.CostEstimate(flops=flops, bytes_accessed=panels.size + current.size * 8, transcendentals=0),
        name="finish",
    )(core, mine, other, panel_factor, own_part, other_part, panels, current)


def couple_kernel(core_ref, gram_ref, weights_ref, out_ref):
    sources, rows, width = gram_ref.shape
    depth = weights_ref.shape[0]
    tiles = depth // 2 // width
    own = rows // tiles
    result = None
    for t in range(tiles):
        gram = gram_ref[:, own * t : own * (t + 1)].reshape(sources * own, width)
        start = pl.multiple_of(core_ref[0] * (depth // 2) + width * t, width)
        term = product(gram, weights_ref[pl.ds(start, width)])
        result = term if result is None else result + term
    out_ref[...] = result


def couple(core, gram, weights):
    return pl.pallas_call(
        couple_kernel,
        out_shape=jax.ShapeDtypeStruct(weights.shape, F32),
        in_specs=[pl.BlockSpec(memory_space=pltpu.SMEM)] + [pl.BlockSpec(memory_space=pltpu.VMEM)] * 2,
        out_specs=pl.BlockSpec(memory_space=pltpu.VMEM),
        cost_estimate=pl.CostEstimate(flops=weights.size * weights.shape[0] * 6, bytes_accessed=gram.size * 4, transcendentals=0),
        name="couple",
    )(core, gram, weights)


def on_device(vectors, band_head, band_tail, band_factor, panel_vectors, panel_factor):
    margin = band_tail.shape[1]
    width = vectors.shape[1]
    depth = panel_factor.shape[1]
    core_index = lax.axis_index("core")
    even = core_index == 0
    core = core_index.astype(jnp.int32).reshape(1)
    n = lax.axis_size(ROW)

    panel_copies = copies(panel_vectors, lax.axis_size("vec"))
    panels = lax.all_to_all(panel_copies, "vec", split_axis=0, concat_axis=0, tiled=True)

    factor = jnp.triu(band_factor[0])
    own = product(band_head, vectors)
    tail = product(band_tail, vectors[:margin])
    cross = product_nt(band_tail, band_head[:, :margin])
    tail_next = lax.ppermute(tail, ROW, [(i + 1, i) for i in range(0, n, 2)])
    weights_a = product(factor, own + tail_next)
    weights_a_prev = lax.ppermute(weights_a, ROW, [(i, i + 1) for i in range(0, n, 2)])
    tail_b = tail - product(cross, weights_a)
    tail_b_next = lax.ppermute(tail_b, ROW, [(i, (i - 1) % n) for i in range(0, n, 2)])
    weights_b = product(factor, own - product_t(cross, weights_a_prev) + tail_b_next)
    weights_b_prev = lax.ppermute(weights_b, ROW, [(i, (i + 1) % n) for i in range(1, n, 2)])
    weights_own = jnp.where(even, weights_a, weights_b)
    weights_prev = jnp.where(even, weights_b_prev, weights_a_prev)
    current = vectors - product_t(band_head, weights_own)
    top = current[:margin] - product_t(band_tail, weights_prev)
    current = jnp.concatenate([top, current[margin:]], axis=0)

    send, keep = project(core, panels, panel_vectors, current)
    group = lax.axis_size("near")
    blocks = (keep + swapped(send)).reshape(group, -1, width)
    share = jnp.sum(lax.all_to_all(blocks, "near", split_axis=0, concat_axis=0, tiled=True), axis=0)
    share = jnp.sum(to_everyone(share, "far"), axis=0)
    mine = to_everyone(share, "near").reshape(-1, width)
    half = depth // 2
    gram_end = mine.shape[0] - half
    gram = to_everyone(mine[half:gram_end], "vec")
    other = swapped(mine)

    weights0 = first_weights(core, mine, other, panel_factor)
    coupled = couple(core, gram, weights0)
    current = apply_first(weights0, panels, current)
    return finish(core, mine, other, panel_factor, coupled, swapped(coupled), panels, current, gram_end)


def solution(mesh):
    devices = mesh.devices.reshape(4, 8, 2, mesh.shape["vec"])
    split = Mesh(devices, ("far", "near", "core", "vec"))
    return jax.shard_map(
        on_device,
        mesh=split,
        in_specs=(
            P(ROW, "vec"),
            P(None, ROW),
            P(None, ROW),
            P(ROW, None, None),
            P(None, "vec", ROW),
            P(),
        ),
        out_specs=P(ROW, "vec"),
        check_vma=False,
    )
```

```python
import functools

import jax
import jax.numpy as jnp
from jax import lax
from jax.experimental import pallas as pl
from jax.experimental.pallas import tpu as pltpu
from jax.sharding import Mesh
from jax.sharding import PartitionSpec as P

HIGHEST = lax.Precision.HIGHEST
F32 = jnp.float32
BF16 = jnp.bfloat16


def product(left, right):
    return jnp.dot(left, right, precision=HIGHEST, preferred_element_type=F32)


def product_t(left, right):
    return lax.dot_general(left, right, (((0,), (0,)), ((), ())), precision=HIGHEST, preferred_element_type=F32)


def product_nt(left, right):
    return lax.dot_general(left, right, (((1,), (1,)), ((), ())), precision=HIGHEST, preferred_element_type=F32)


def store_pieces(target, array):
    width = array.shape[1]
    high = array.astype(BF16)
    target[:, :width] = high
    target[:, width:] = (array - high.astype(F32)).astype(BF16)


def fold(wide):
    width = wide.shape[1] // 2
    return wide[:, :width] + wide[:, width:]


def exchanged(blocks, axis, groups=None):
    return lax.all_to_all(blocks, axis, split_axis=0, concat_axis=0, tiled=True, axis_index_groups=groups)


def to_everyone(array, axis, groups=None):
    members = lax.axis_size(axis) if groups is None else len(groups[0])
    return exchanged(jnp.broadcast_to(array, (members, *array.shape)), axis, groups)


def swapped(array):
    return lax.ppermute(array, "row", [(i, i ^ 1) for i in range(lax.axis_size("row"))])


def row_groups(devices):
    chips = devices // 2
    far = min(4, chips // 2)
    near = chips // far
    at = lambda core, f, p: 2 * ((near * f + near // 2 * core + p) % chips) + core
    near_groups = [[at(core, f, p) for p in range(near)] for core in range(2) for f in range(far)]
    far_groups = [[at(core, f, p) for f in range(far)] for core in range(2) for p in range(near)]
    return near_groups, far_groups


def copies_kernel(source_ref, out_ref, sems):
    moves = [pltpu.make_async_copy(source_ref, out_ref.at[i], sems.at[i]) for i in range(out_ref.shape[0])]
    for move in moves:
        move.start()
    for move in moves:
        move.wait()


def copies(array, count):
    return pl.pallas_call(
        copies_kernel,
        out_shape=jax.ShapeDtypeStruct((count, *array.shape), array.dtype),
        in_specs=[pl.BlockSpec(memory_space=pltpu.VMEM)],
        out_specs=pl.BlockSpec(memory_space=pl.ANY),
        scratch_shapes=[pltpu.SemaphoreType.DMA((count,))],
        name="copies",
    )(array)


def project_kernel(core_ref, panel_ref, own_ref, current_ref, after_ref, send_ref, keep_ref, split):
    del core_ref, after_ref
    step = pl.program_id(0)

    @pl.when(step == 0)
    def _():
        store_pieces(split, current_ref[...])

    rows = panel_ref.shape[0] * panel_ref.shape[1]
    own, width = own_ref.shape[0], current_ref.shape[1]
    tiles = rows // width
    gram_end = rows + own * tiles
    panel = panel_ref[...].reshape(rows, panel_ref.shape[2])
    part = fold(jnp.dot(panel, split[...], preferred_element_type=F32))
    for which, out_ref in enumerate((send_ref, keep_ref)):

        @pl.when(step == 2 * which)
        def _(out_ref=out_ref):
            out_ref[:rows] = part
            gram = lax.dot_general(own_ref[...], panel, (((1,), (1,)), ((), ())), preferred_element_type=F32)
            for t in range(tiles):
                out_ref[rows + own * t : rows + own * (t + 1)] = gram[:, width * t : width * (t + 1)]

        @pl.when(step == 2 * which + 1)
        def _(out_ref=out_ref):
            out_ref[gram_end:] = part


def project(core, panels, panel_vectors, current, after):
    sources, _, own, depth_rows = panels.shape
    rows, width = sources // 2 * own, current.shape[1]
    total = 2 * rows + own * (rows // width)
    whole = pl.BlockSpec((total, width), lambda i, c: (0, 0))
    flops = 2 * 2 * sources * own * depth_rows * width * 2
    return pl.pallas_call(
        project_kernel,
        out_shape=[jax.ShapeDtypeStruct((total, width), F32)] * 2,
        grid_spec=pltpu.PrefetchScalarGridSpec(
            num_scalar_prefetch=1,
            grid=(4,),
            in_specs=[
                pl.BlockSpec(
                    (sources // 2, None, own, depth_rows),
                    lambda i, c: (jnp.where(i < 2, 1 - c[0], c[0]), i % 2, 0, 0),
                ),
                pl.BlockSpec((None, own, depth_rows), lambda i, c: (1, 0, 0)),
                pl.BlockSpec(current.shape, lambda i, c: (0, 0)),
                pl.BlockSpec(memory_space=pl.ANY),
            ],
            out_specs=[whole, whole],
            scratch_shapes=[pltpu.VMEM((depth_rows, 2 * width), BF16)],
        ),
        cost_estimate=pl.CostEstimate(flops=flops, bytes_accessed=panels.size * 2 + current.size * 4, transcendentals=0),
        name="project",
    )(core, panels, panel_vectors, current, after)


def prepare_kernel(factor_ref, out_ref):
    depth = factor_ref.shape[0]
    row = lax.broadcasted_iota(jnp.int32, (depth, depth), 0)
    column = lax.broadcasted_iota(jnp.int32, (depth, depth), 1)
    store_pieces(out_ref, jnp.where(row <= column, factor_ref[...], 0.0))


def prepare(panel_factor):
    count, depth, _ = panel_factor.shape
    return pl.pallas_call(
        prepare_kernel,
        out_shape=jax.ShapeDtypeStruct((count, depth, 2 * depth), BF16),
        grid=(count,),
        in_specs=[pl.BlockSpec((None, depth, depth), lambda i: (i, 0, 0))],
        out_specs=pl.BlockSpec((None, depth, 2 * depth), lambda i: (i, 0, 0)),
        cost_estimate=pl.CostEstimate(flops=panel_factor.size, bytes_accessed=panel_factor.size * 8, transcendentals=0),
        name="prepare",
    )(panel_factor)


def in_pieces(left_high, left_low, right):
    width = right.shape[1] // 2
    main = jnp.dot(left_high, right, preferred_element_type=F32)
    return fold(main) + jnp.dot(left_low, right[:, :width], preferred_element_type=F32)


def weigh(first_row, core_ref, mine_ref, other_ref, factor_ref, total, split, corrections=()):
    depth = factor_ref.shape[0]
    half = depth // 2
    for which, (low_ref, high_ref) in enumerate(((mine_ref, other_ref), (other_ref, mine_ref))):

        @pl.when(core_ref[0] == which)
        def _(low_ref=low_ref, high_ref=high_ref):
            total[:half] = low_ref[first_row : first_row + half]
            total[half:] = high_ref[first_row : first_row + half]

    wanted = total[...]
    if corrections:
        wanted = wanted - (corrections[0][...] + corrections[1][...])
    store_pieces(split, wanted)
    return in_pieces(factor_ref[:, :depth], factor_ref[:, depth:], split[...])


def first_weights_kernel(core_ref, mine_ref, other_ref, factor_ref, weights_ref, total, split):
    store_pieces(weights_ref, weigh(0, core_ref, mine_ref, other_ref, factor_ref, total, split))


def first_weights(core, mine, other, factors):
    depth, width = factors.shape[1], mine.shape[1]
    whole = pl.BlockSpec(mine.shape, lambda i, c: (0, 0))
    return pl.pallas_call(
        first_weights_kernel,
        out_shape=jax.ShapeDtypeStruct((depth, 2 * width), BF16),
        grid_spec=pltpu.PrefetchScalarGridSpec(
            num_scalar_prefetch=1,
            grid=(1,),
            in_specs=[whole, whole, pl.BlockSpec((None, depth, 2 * depth), lambda i, c: (0, 0, 0))],
            out_specs=pl.BlockSpec((depth, 2 * width), lambda i, c: (0, 0)),
            scratch_shapes=[pltpu.VMEM((depth, width), F32), pltpu.VMEM((depth, 2 * width), BF16)],
        ),
        cost_estimate=pl.CostEstimate(flops=2 * depth * depth * width * 3, bytes_accessed=4 * depth * depth, transcendentals=0),
        name="first_weights",
    )(core, mine, other, factors)


def update(panel_ref, split, current_ref, out_ref):
    panel = panel_ref[...].reshape(split.shape[0], panel_ref.shape[2])
    wide = lax.dot_general(panel, split[...], (((0,), (0,)), ((), ())), preferred_element_type=F32)
    out_ref[...] = current_ref[...] - fold(wide)


def apply_kernel(weights_ref, panel_ref, current_ref, out_ref):
    update(panel_ref, weights_ref, current_ref, out_ref)


STEPS = 4


def apply_first(weights, panels, current):
    sources, _, own, n_rows = panels.shape
    depth, width = weights.shape[0], current.shape[1]
    block = n_rows // STEPS
    rows = pl.BlockSpec((block, width), lambda i: (i, 0))
    return pl.pallas_call(
        apply_kernel,
        out_shape=jax.ShapeDtypeStruct(current.shape, F32),
        grid=(STEPS,),
        in_specs=[
            pl.BlockSpec(weights.shape, lambda i: (0, 0)),
            pl.BlockSpec((sources, None, own, block), lambda i: (0, 0, 0, i)),
            rows,
        ],
        out_specs=rows,
        cost_estimate=pl.CostEstimate(
            flops=2 * n_rows * depth * width * 2, bytes_accessed=panels.size + current.size * 8, transcendentals=0
        ),
        name="apply_first",
    )(weights, panels, current)


def finish_kernel(
    first_row, core_ref, mine_ref, other_ref, factor_ref, own_part, other_part, panel_ref, current_ref, out_ref, total, split
):
    @pl.when(pl.program_id(0) == 0)
    def _():
        corrections = (own_part, other_part)
        store_pieces(split, weigh(first_row, core_ref, mine_ref, other_ref, factor_ref, total, split, corrections))

    update(panel_ref, split, current_ref, out_ref)


def finish(core, mine, other, factors, own_part, other_part, panels, current, first_row):
    sources, _, own, n_rows = panels.shape
    depth, width = own_part.shape
    block = n_rows // STEPS
    whole = lambda array: pl.BlockSpec(array.shape, lambda i, c: (0, 0))
    rows = pl.BlockSpec((block, width), lambda i, c: (i, 0))
    flops = 2 * n_rows * depth * width * 2 + 2 * depth * depth * width * 3
    return pl.pallas_call(
        functools.partial(finish_kernel, first_row),
        out_shape=jax.ShapeDtypeStruct(current.shape, F32),
        grid_spec=pltpu.PrefetchScalarGridSpec(
            num_scalar_prefetch=1,
            grid=(STEPS,),
            in_specs=[
                whole(mine),
                whole(other),
                pl.BlockSpec((None, depth, 2 * depth), lambda i, c: (1, 0, 0)),
                whole(own_part),
                whole(other_part),
                pl.BlockSpec((sources, None, own, block), lambda i, c: (0, 1, 0, i)),
                rows,
            ],
            out_specs=rows,
            scratch_shapes=[pltpu.VMEM((depth, width), F32), pltpu.VMEM((depth, 2 * width), BF16)],
        ),
        cost_estimate=pl.CostEstimate(flops=flops, bytes_accessed=panels.size + current.size * 8, transcendentals=0),
        name="finish",
    )(core, mine, other, factors, own_part, other_part, panels, current)


def couple_kernel(core_ref, gram_ref, weights_ref, after_ref, out_ref):
    del after_ref
    sources, rows, width = gram_ref.shape
    half = weights_ref.shape[0] // 2
    tiles = half // width
    own = rows // tiles
    result = None
    for t in range(tiles):
        gram = gram_ref[:, own * t : own * (t + 1)].reshape(sources * own, width)
        high = gram.astype(BF16)
        low = (gram - high.astype(F32)).astype(BF16)
        start = pl.multiple_of(core_ref[0] * half + width * t, width)
        term = in_pieces(high, low, weights_ref[pl.ds(start, width)])
        result = term if result is None else result + term
    out_ref[...] = result


def couple(core, gram, weights, after):
    depth, width = weights.shape[0], weights.shape[1] // 2
    return pl.pallas_call(
        couple_kernel,
        out_shape=jax.ShapeDtypeStruct((depth, width), F32),
        in_specs=[
            pl.BlockSpec(memory_space=pltpu.SMEM),
            pl.BlockSpec(memory_space=pltpu.VMEM),
            pl.BlockSpec(memory_space=pltpu.VMEM),
            pl.BlockSpec(memory_space=pl.ANY),
        ],
        out_specs=pl.BlockSpec(memory_space=pltpu.VMEM),
        cost_estimate=pl.CostEstimate(flops=depth * depth * width * 3, bytes_accessed=gram.size * 4, transcendentals=0),
        name="couple",
    )(core, gram, weights, after)


def on_device(vectors, band_head, band_tail, band_factor, panel_vectors, panel_factor):
    margin = band_tail.shape[1]
    width = vectors.shape[1]
    depth = panel_factor.shape[1]
    core_index = lax.axis_index("row") % 2
    even = core_index == 0
    core = core_index.astype(jnp.int32).reshape(1)
    n = lax.axis_size("row")
    near_groups, far_groups = row_groups(n)

    panel_copies = copies(panel_vectors, lax.axis_size("vec"))
    panels = exchanged(panel_copies, "vec")

    factors = prepare(panel_factor)
    factor = jnp.triu(band_factor[0])
    own = product(band_head, vectors)
    tail = product(band_tail, vectors[:margin])
    cross = product_nt(band_tail, band_head[:, :margin])
    tail_next = lax.ppermute(tail, "row", [(i + 1, i) for i in range(0, n, 2)])
    weights_a = product(factor, own + tail_next)
    weights_a_prev = lax.ppermute(weights_a, "row", [(i, i + 1) for i in range(0, n, 2)])
    tail_b = tail - product(cross, weights_a)
    tail_b_next = lax.ppermute(tail_b, "row", [(i, (i - 1) % n) for i in range(0, n, 2)])
    weights_b = product(factor, own - product_t(cross, weights_a_prev) + tail_b_next)
    weights_b_prev = lax.ppermute(weights_b, "row", [(i, (i + 1) % n) for i in range(1, n, 2)])
    weights_own = jnp.where(even, weights_a, weights_b)
    weights_prev = jnp.where(even, weights_b_prev, weights_a_prev)
    current = vectors - product_t(band_head, weights_own)
    top = current[:margin] - product_t(band_tail, weights_prev)
    current = jnp.concatenate([top, current[margin:]], axis=0)

    send, keep = project(core, panels, panel_vectors, current, factors)
    blocks = (keep + swapped(send)).reshape(len(near_groups[0]), -1, width)
    share = jnp.sum(exchanged(blocks, "row", near_groups), axis=0)
    share = jnp.sum(to_everyone(share, "row", far_groups), axis=0)
    mine = to_everyone(share, "row", near_groups).reshape(-1, width)
    half = depth // 2
    gram_end = mine.shape[0] - half
    gram = to_everyone(mine[half:gram_end], "vec")
    other = swapped(mine)

    weights0 = first_weights(core, mine, other, factors)
    current = apply_first(weights0, panels, current)
    coupled = couple(core, gram, weights0, current)
    return finish(core, mine, other, factors, coupled, swapped(coupled), panels, current, gram_end)


def solution(mesh):
    return jax.shard_map(
        on_device,
        mesh=mesh,
        in_specs=(
            P("row", "vec"),
            P(None, "row"),
            P(None, "row"),
            P("row", None, None),
            P(None, "vec", "row"),
            P(),
        ),
        out_specs=P("row", "vec"),
        check_vma=False,
    )
```

```python
import functools

import jax
import jax.numpy as jnp
from jax import lax
from jax.experimental import pallas as pl
from jax.experimental.pallas import tpu as pltpu
from jax.sharding import Mesh
from jax.sharding import PartitionSpec as P

HIGHEST = lax.Precision.HIGHEST
F32 = jnp.float32
BF16 = jnp.bfloat16


def product(left, right):
    return jnp.dot(left, right, precision=HIGHEST, preferred_element_type=F32)


def product_t(left, right):
    return lax.dot_general(left, right, (((0,), (0,)), ((), ())), precision=HIGHEST, preferred_element_type=F32)


def product_nt(left, right):
    return lax.dot_general(left, right, (((1,), (1,)), ((), ())), precision=HIGHEST, preferred_element_type=F32)


def store_pieces(target, array):
    width = array.shape[1]
    high = array.astype(BF16)
    target[:, :width] = high
    target[:, width:] = (array - high.astype(F32)).astype(BF16)


def fold(wide):
    width = wide.shape[1] // 2
    return wide[:, :width] + wide[:, width:]


def exchanged(blocks, axis, groups=None):
    return lax.all_to_all(blocks, axis, split_axis=0, concat_axis=0, tiled=True, axis_index_groups=groups)


def to_everyone(array, axis, groups=None):
    members = lax.axis_size(axis) if groups is None else len(groups[0])
    return exchanged(jnp.broadcast_to(array, (members, *array.shape)), axis, groups)


def swapped(array):
    return lax.ppermute(array, "row", [(i, i ^ 1) for i in range(lax.axis_size("row"))])


def row_groups(devices):
    chips = devices // 2
    far = min(4, chips // 2)
    near = chips // far
    at = lambda core, f, p: 2 * ((near * f + near // 2 * core + p) % chips) + core
    near_groups = [[at(core, f, p) for p in range(near)] for core in range(2) for f in range(far)]
    far_groups = [[at(core, f, p) for f in range(far)] for core in range(2) for p in range(near)]
    return near_groups, far_groups


def copies_kernel(index, source_ref, *refs):
    out_ref, sems = refs[-2:]
    moves = [
        pltpu.make_async_copy(source_ref.at[index], out_ref.at[i], sems.at[i]) for i in range(out_ref.shape[0])
    ]
    for move in moves:
        move.start()
    for move in moves:
        move.wait()


def copies(array, index, count, after=()):
    return pl.pallas_call(
        functools.partial(copies_kernel, index),
        out_shape=jax.ShapeDtypeStruct((count, *array.shape[1:]), array.dtype),
        in_specs=[pl.BlockSpec(memory_space=pltpu.VMEM)] + [pl.BlockSpec(memory_space=pl.ANY)] * len(after),
        out_specs=pl.BlockSpec(memory_space=pl.ANY),
        scratch_shapes=[pltpu.SemaphoreType.DMA((count,))],
        compiler_params=pltpu.CompilerParams(vmem_limit_bytes=8 << 20 if after else None),
        name="copies",
    )(array, *after)


def project_kernel(core_ref, panel0_ref, panel1_ref, own_ref, current_ref, after_ref, send_ref, keep_ref, split):
    del core_ref, after_ref
    step = pl.program_id(0)

    @pl.when(step == 0)
    def _():
        store_pieces(split, current_ref[...])

    rows = panel0_ref.shape[0] * panel0_ref.shape[1]
    own, width = own_ref.shape[0], current_ref.shape[1]
    tiles = rows // width
    panel0 = panel0_ref[...].reshape(rows, panel0_ref.shape[2])
    panel1 = panel1_ref[...].reshape(rows, panel1_ref.shape[2])
    part0 = fold(jnp.dot(panel0, split[...], preferred_element_type=F32))
    part1 = fold(jnp.dot(panel1, split[...], preferred_element_type=F32))
    gram = lax.dot_general(own_ref[...], panel0, (((1,), (1,)), ((), ())), preferred_element_type=F32)
    for which, out_ref in enumerate((send_ref, keep_ref)):

        @pl.when(step == which)
        def _(out_ref=out_ref):
            out_ref[:rows] = part0
            for t in range(tiles):
                out_ref[rows + own * t : rows + own * (t + 1)] = gram[:, width * t : width * (t + 1)]
            out_ref[rows + own * tiles :] = part1


def project(core, panel0, panel1, panel_vectors, current, after):
    sources, own, depth_rows = panel0.shape
    rows, width = sources // 2 * own, current.shape[1]
    total = 2 * rows + own * (rows // width)
    whole = pl.BlockSpec((total, width), lambda i, c: (0, 0))
    half = pl.BlockSpec((sources // 2, own, depth_rows), lambda i, c: (jnp.where(i == 0, 1 - c[0], c[0]), 0, 0))
    flops = 2 * 2 * sources * own * depth_rows * width * 2
    return pl.pallas_call(
        project_kernel,
        out_shape=[jax.ShapeDtypeStruct((total, width), F32)] * 2,
        grid_spec=pltpu.PrefetchScalarGridSpec(
            num_scalar_prefetch=1,
            grid=(2,),
            in_specs=[
                half,
                half,
                pl.BlockSpec((None, own, depth_rows), lambda i, c: (1, 0, 0)),
                pl.BlockSpec(current.shape, lambda i, c: (0, 0)),
                pl.BlockSpec(memory_space=pl.ANY),
            ],
            out_specs=[whole, whole],
            scratch_shapes=[pltpu.VMEM((depth_rows, 2 * width), BF16)],
        ),
        compiler_params=pltpu.CompilerParams(vmem_limit_bytes=24 << 20),
        cost_estimate=pl.CostEstimate(flops=flops, bytes_accessed=panel0.size * 4 + current.size * 4, transcendentals=0),
        name="project",
    )(core, panel0, panel1, panel_vectors, current, after)


def prepare_kernel(factor_ref, out_ref):
    depth = factor_ref.shape[0]
    row = lax.broadcasted_iota(jnp.int32, (depth, depth), 0)
    column = lax.broadcasted_iota(jnp.int32, (depth, depth), 1)
    store_pieces(out_ref, jnp.where(row <= column, factor_ref[...], 0.0))


def prepare(panel_factor):
    count, depth, _ = panel_factor.shape
    return pl.pallas_call(
        prepare_kernel,
        out_shape=jax.ShapeDtypeStruct((count, depth, 2 * depth), BF16),
        grid=(count,),
        in_specs=[pl.BlockSpec((None, depth, depth), lambda i: (i, 0, 0))],
        out_specs=pl.BlockSpec((None, depth, 2 * depth), lambda i: (i, 0, 0)),
        cost_estimate=pl.CostEstimate(flops=panel_factor.size, bytes_accessed=panel_factor.size * 8, transcendentals=0),
        name="prepare",
    )(panel_factor)


def in_pieces(left_high, left_low, right):
    width = right.shape[1] // 2
    main = jnp.dot(left_high, right, preferred_element_type=F32)
    return fold(main) + jnp.dot(left_low, right[:, :width], preferred_element_type=F32)


def weigh(first_row, core_ref, mine_ref, other_ref, factor_ref, total, split, corrections=()):
    depth = factor_ref.shape[0]
    half = depth // 2
    for which, (low_ref, high_ref) in enumerate(((mine_ref, other_ref), (other_ref, mine_ref))):

        @pl.when(core_ref[0] == which)
        def _(low_ref=low_ref, high_ref=high_ref):
            total[:half] = low_ref[first_row : first_row + half]
            total[half:] = high_ref[first_row : first_row + half]

    wanted = total[...]
    if corrections:
        wanted = wanted - (corrections[0][...] + corrections[1][...])
    store_pieces(split, wanted)
    return in_pieces(factor_ref[:, :depth], factor_ref[:, depth:], split[...])


def first_weights_kernel(core_ref, mine_ref, other_ref, factor_ref, weights_ref, total, split):
    store_pieces(weights_ref, weigh(0, core_ref, mine_ref, other_ref, factor_ref, total, split))


def first_weights(core, mine, other, factors):
    depth, width = factors.shape[1], mine.shape[1]
    whole = pl.BlockSpec(mine.shape, lambda i, c: (0, 0))
    return pl.pallas_call(
        first_weights_kernel,
        out_shape=jax.ShapeDtypeStruct((depth, 2 * width), BF16),
        grid_spec=pltpu.PrefetchScalarGridSpec(
            num_scalar_prefetch=1,
            grid=(1,),
            in_specs=[whole, whole, pl.BlockSpec((None, depth, 2 * depth), lambda i, c: (0, 0, 0))],
            out_specs=pl.BlockSpec((depth, 2 * width), lambda i, c: (0, 0)),
            scratch_shapes=[pltpu.VMEM((depth, width), F32), pltpu.VMEM((depth, 2 * width), BF16)],
        ),
        cost_estimate=pl.CostEstimate(flops=2 * depth * depth * width * 3, bytes_accessed=4 * depth * depth, transcendentals=0),
        name="first_weights",
    )(core, mine, other, factors)


def update(panel_ref, split, current_ref, out_ref):
    panel = panel_ref[...].reshape(split.shape[0], panel_ref.shape[2])
    wide = lax.dot_general(panel, split[...], (((0,), (0,)), ((), ())), preferred_element_type=F32)
    out_ref[...] = current_ref[...] - fold(wide)


def apply_kernel(weights_ref, panel_ref, current_ref, out_ref):
    update(panel_ref, weights_ref, current_ref, out_ref)


STEPS = 4


def apply_first(weights, panel, current):
    sources, own, n_rows = panel.shape
    depth, width = weights.shape[0], current.shape[1]
    block = n_rows // STEPS
    rows = pl.BlockSpec((block, width), lambda i: (i, 0))
    return pl.pallas_call(
        apply_kernel,
        out_shape=jax.ShapeDtypeStruct(current.shape, F32),
        grid=(STEPS,),
        in_specs=[
            pl.BlockSpec(weights.shape, lambda i: (0, 0)),
            pl.BlockSpec((sources, own, block), lambda i: (0, 0, i)),
            rows,
        ],
        out_specs=rows,
        cost_estimate=pl.CostEstimate(
            flops=2 * n_rows * depth * width * 2, bytes_accessed=panel.size * 2 + current.size * 8, transcendentals=0
        ),
        name="apply_first",
    )(weights, panel, current)


def finish_kernel(
    first_row, core_ref, mine_ref, other_ref, factor_ref, own_part, other_part, panel_ref, current_ref, out_ref, total, split
):
    @pl.when(pl.program_id(0) == 0)
    def _():
        corrections = (own_part, other_part)
        store_pieces(split, weigh(first_row, core_ref, mine_ref, other_ref, factor_ref, total, split, corrections))

    update(panel_ref, split, current_ref, out_ref)


def finish(core, mine, other, factors, own_part, other_part, panel, current, first_row):
    sources, own, n_rows = panel.shape
    depth, width = own_part.shape
    block = n_rows // STEPS
    whole = lambda array: pl.BlockSpec(array.shape, lambda i, c: (0, 0))
    rows = pl.BlockSpec((block, width), lambda i, c: (i, 0))
    flops = 2 * n_rows * depth * width * 2 + 2 * depth * depth * width * 3
    return pl.pallas_call(
        functools.partial(finish_kernel, first_row),
        out_shape=jax.ShapeDtypeStruct(current.shape, F32),
        grid_spec=pltpu.PrefetchScalarGridSpec(
            num_scalar_prefetch=1,
            grid=(STEPS,),
            in_specs=[
                whole(mine),
                whole(other),
                pl.BlockSpec((None, depth, 2 * depth), lambda i, c: (1, 0, 0)),
                whole(own_part),
                whole(other_part),
                pl.BlockSpec((sources, own, block), lambda i, c: (0, 0, i)),
                rows,
            ],
            out_specs=rows,
            scratch_shapes=[pltpu.VMEM((depth, width), F32), pltpu.VMEM((depth, 2 * width), BF16)],
        ),
        cost_estimate=pl.CostEstimate(flops=flops, bytes_accessed=panel.size * 2 + current.size * 8, transcendentals=0),
        name="finish",
    )(core, mine, other, factors, own_part, other_part, panel, current)


def couple_kernel(core_ref, gram_ref, weights_ref, after_ref, out_ref):
    del after_ref
    sources, rows, width = gram_ref.shape
    half = weights_ref.shape[0] // 2
    tiles = half // width
    own = rows // tiles
    result = None
    for t in range(tiles):
        gram = gram_ref[:, own * t : own * (t + 1)].reshape(sources * own, width)
        high = gram.astype(BF16)
        low = (gram - high.astype(F32)).astype(BF16)
        start = pl.multiple_of(core_ref[0] * half + width * t, width)
        term = in_pieces(high, low, weights_ref[pl.ds(start, width)])
        result = term if result is None else result + term
    out_ref[...] = result


def couple(core, gram, weights, after):
    depth, width = weights.shape[0], weights.shape[1] // 2
    return pl.pallas_call(
        couple_kernel,
        out_shape=jax.ShapeDtypeStruct((depth, width), F32),
        in_specs=[
            pl.BlockSpec(memory_space=pltpu.SMEM),
            pl.BlockSpec(memory_space=pltpu.VMEM),
            pl.BlockSpec(memory_space=pltpu.VMEM),
            pl.BlockSpec(memory_space=pl.ANY),
        ],
        out_specs=pl.BlockSpec(memory_space=pltpu.VMEM),
        cost_estimate=pl.CostEstimate(flops=depth * depth * width * 3, bytes_accessed=gram.size * 4, transcendentals=0),
        name="couple",
    )(core, gram, weights, after)


def on_device(vectors, band_head, band_tail, band_factor, panel_vectors, panel_factor):
    margin = band_tail.shape[1]
    width = vectors.shape[1]
    depth = panel_factor.shape[1]
    core_index = lax.axis_index("row") % 2
    even = core_index == 0
    core = core_index.astype(jnp.int32).reshape(1)
    n = lax.axis_size("row")
    near_groups, far_groups = row_groups(n)

    vec = lax.axis_size("vec")
    vectors, panel0_copies = lax.optimization_barrier((vectors, copies(panel_vectors, 0, vec)))
    panel0 = exchanged(panel0_copies, "vec")

    factors = prepare(panel_factor)
    factor = jnp.triu(band_factor[0])
    own = product(band_head, vectors)
    tail = product(band_tail, vectors[:margin])
    cross = product_nt(band_tail, band_head[:, :margin])
    tail_next = lax.ppermute(tail, "row", [(i + 1, i) for i in range(0, n, 2)])
    weights_a = product(factor, own + tail_next)
    weights_a_prev = lax.ppermute(weights_a, "row", [(i, i + 1) for i in range(0, n, 2)])
    tail_b = tail - product(cross, weights_a)
    tail_b_next = lax.ppermute(tail_b, "row", [(i, (i - 1) % n) for i in range(0, n, 2)])
    weights_b = product(factor, own - product_t(cross, weights_a_prev) + tail_b_next)
    weights_b_prev = lax.ppermute(weights_b, "row", [(i, (i + 1) % n) for i in range(1, n, 2)])
    weights_own = jnp.where(even, weights_a, weights_b)
    weights_prev = jnp.where(even, weights_b_prev, weights_a_prev)
    current = vectors - product_t(band_head, weights_own)
    top = current[:margin] - product_t(band_tail, weights_prev)
    current = jnp.concatenate([top, current[margin:]], axis=0)

    panel1 = exchanged(copies(panel_vectors, 1, vec, (current, factors)), "vec")
    send, keep = project(core, panel0, panel1, panel_vectors, current, factors)
    blocks = (keep + swapped(send)).reshape(len(near_groups[0]), -1, width)
    share = jnp.sum(exchanged(blocks, "row", near_groups), axis=0)
    share = jnp.sum(to_everyone(share, "row", far_groups), axis=0)
    mine = to_everyone(share, "row", near_groups).reshape(-1, width)
    half = depth // 2
    gram_end = mine.shape[0] - half
    gram = to_everyone(mine[half:gram_end], "vec")
    other = swapped(mine)

    weights0 = first_weights(core, mine, other, factors)
    current = apply_first(weights0, panel0, current)
    coupled = couple(core, gram, weights0, current)
    return finish(core, mine, other, factors, coupled, swapped(coupled), panel1, current, gram_end)


def solution(mesh):
    return jax.shard_map(
        on_device,
        mesh=mesh,
        in_specs=(
            P("row", "vec"),
            P(None, "row"),
            P(None, "row"),
            P("row", None, None),
            P(None, "vec", "row"),
            P(),
        ),
        out_specs=P("row", "vec"),
        check_vma=False,
    )
```
